32 devices in a mesh: shot: 2 (over core), gy: 4 (over y, x), gx: 4 (over z).
Axes of the slice: x: 2, y: 2, z: 4, core: 2. Of those that a mesh axis runs over, the one named last changes fastest.
Arguments:
- fwd_prev: float32 [2, 4, 1024, 512], P('shot', None, 'gy', 'gx'), may hold values from -6 to 6
- fwd_cur: float32 [2, 4, 1024, 512], P('shot', None, 'gy', 'gx'), may hold values from -6 to 6
- adj_late: float32 [2, 4, 1024, 512], P('shot', None, 'gy', 'gx'), may hold values from -6 to 6
- adj_now: float32 [2, 4, 1024, 512], P('shot', None, 'gy', 'gx'), may hold values from -6 to 6
- courant: float32 [4, 1024, 512], P(None, 'gy', 'gx'), may hold values from 0.02 to 0.19
- wavelet: float32 [2, 2], P('shot'), may hold values from -16 to 16
- boxes: int32 [2, 4], P('shot'), may hold values from 0 to 1024, as said below
- sources: int32 [2, 3], P('shot'), may hold values from 0 to 1023, as said below
- slab_top: int32 [1], replicated, may hold values from 0 to 508
Outputs:
- gradient: float32 [2, 512, 256], P(None, 'gy', 'gx')
The draws below stay inside these ranges and needn't reach their ends.
Inputs may be any that keep to these rules, and one draw needn't show every extreme that they name: `boxes`: shot s's box is y0 <= y < y1, x0 <= x < x1 with y0 < y1 <= 1024, x0 < x1 <= 512, every bound a multiple of 16. `sources`: each shot's source cell (z, y, x) lies in the slab and inside that shot's box.
All inputs are finite; a program needn't handle non-finite values.
Results may differ from the reference program's by a relative error of at most 0.0003.
Values sent between devices are 32-bit elements; how exact they have to be, the bound alone decides.
A program may use at most 128 MiB of HBM per device.

```python
import math
import jax
import jax.numpy as jnp
from jax import lax

BLK = 16
DEPTH = 512
SHOTS = 2
NZ = 4
NY = 1024
NX = 512


def boxes_and_sources(key):
    base_key = jax.random.fold_in(key, 7)
    sub_keys = jax.random.split(base_key, 8)
    blocks_y = NY // BLK
    blocks_x = NX // BLK
    length_y = jax.random.randint(sub_keys[0], (SHOTS,), max(1, blocks_y // 4), blocks_y + 1)
    length_x = jax.random.randint(sub_keys[1], (SHOTS,), max(1, blocks_x // 4), blocks_x + 1)
    widest = jax.random.randint(sub_keys[2], (), 0, SHOTS)
    is_widest = jnp.arange(SHOTS) == widest
    length_y = jnp.where(is_widest, blocks_y, length_y)
    length_x = jnp.where(is_widest, blocks_x, length_x)
    start_y = jax.random.randint(sub_keys[3], (SHOTS,), 0, 1 << 20) % (blocks_y - length_y + 1)
    start_x = jax.random.randint(sub_keys[4], (SHOTS,), 0, 1 << 20) % (blocks_x - length_x + 1)
    low_y = start_y * BLK
    high_y = (start_y + length_y) * BLK
    low_x = start_x * BLK
    high_x = (start_x + length_x) * BLK
    source_y = low_y + jax.random.randint(sub_keys[5], (SHOTS,), 0, 1 << 20) % (high_y - low_y)
    source_x = low_x + jax.random.randint(sub_keys[6], (SHOTS,), 0, 1 << 20) % (high_x - low_x)
    source_z = jax.random.randint(sub_keys[7], (SHOTS,), 0, NZ)
    source_y = jnp.where(is_widest, NY - 1, source_y)
    source_x = jnp.where(is_widest, NX - 1, source_x)
    source_z = jnp.where(is_widest, 0, source_z)
    box_table = jnp.stack([low_y, high_y, low_x, high_x], axis=1).astype(jnp.int32)
    source_table = jnp.stack([source_z, source_y, source_x], axis=1).astype(jnp.int32)
    return (box_table, source_table)


def draw_boxes(key, part):
    return boxes_and_sources(key)[0]


def draw_sources(key, part):
    return boxes_and_sources(key)[1]


def wave_field(key, tag):
    shape = (SHOTS, NZ, NY, NX)
    rough_key = jax.random.fold_in(key, tag)
    return jnp.clip(jax.random.normal(rough_key, shape, jnp.float32), -6.0, 6.0)


def draw_fwd_prev(key, part):
    return wave_field(key, 11)


def draw_fwd_cur(key, part):
    return wave_field(key, 12)


def draw_adj_late(key, part):
    return wave_field(key, 13)


def draw_adj_now(key, part):
    return wave_field(key, 14)


def block_levels(own_key, dims, shards, least, largest):
    factor_of = 1.0
    for axis_at, shards_of in shards:
        draws = jax.random.uniform(jax.random.fold_in(jax.random.fold_in(own_key, 6), axis_at), (shards_of,), jnp.float32, least / len(shards), largest / len(shards))
        factor_of = factor_of * jnp.repeat(jnp.exp(draws), dims[axis_at] // shards_of).reshape((-1,) + (1,) * (len(dims) - 1 - axis_at))
    return factor_of


def noise(key, dims, width, most, cuts=(), held_as=jnp.bfloat16):
    entries = jax.random.normal(key, dims, jnp.float32) * width
    if len(cuts) > 0:
        entries = block_levels(key, dims, cuts, -0.22, 0.18) * entries
    return jnp.clip(entries, min=-most, max=most).astype(held_as)


def setup_inputs(seed: int = 0) -> dict:
    key_of = jax.random.split(jax.random.key(seed), 10)
    return {
        "fwd_prev": draw_fwd_prev(jax.random.fold_in(key_of[9], 71), 0),
        "fwd_cur": draw_fwd_cur(jax.random.fold_in(key_of[9], 71), 0),
        "adj_late": draw_adj_late(jax.random.fold_in(key_of[9], 71), 0),
        "adj_now": draw_adj_now(jax.random.fold_in(key_of[9], 71), 0),
        "courant": jnp.clip(jnp.exp(math.log(0.19) - 2.2512918 * jax.random.uniform(key_of[4], (NZ, NY, NX), jnp.float32) ** block_levels(key_of[4], (NZ, NY, NX), ((1, 4), (2, 4)), -0.2, 0.2)), 0.02, 0.19),
        "wavelet": noise(key_of[5], (SHOTS, 2), 4.0, 16.0, ((0, 2),), jnp.float32),
        "boxes": draw_boxes(jax.random.fold_in(key_of[9], 71), 0),
        "sources": draw_sources(jax.random.fold_in(key_of[9], 71), 0),
        "slab_top": jax.random.randint(key_of[8], (1,), 0, DEPTH - NZ + 1).astype(jnp.int32),
    }


COEFFS = (-205.0 / 72.0, 8.0 / 5.0, -1.0 / 5.0, 8.0 / 315.0, -1.0 / 560.0)


def laplace(field):
    padded = jnp.pad(field, 4)
    depth_count, span_y, span_x = field.shape
    summed = 3.0 * COEFFS[0] * field
    for offset in range(1, 5):
        neighbours = padded[4 + offset:4 + offset + depth_count, 4:4 + span_y, 4:4 + span_x]
        neighbours = neighbours + padded[4 - offset:4 - offset + depth_count, 4:4 + span_y, 4:4 + span_x]
        neighbours = neighbours + padded[4:4 + depth_count, 4 + offset:4 + offset + span_y, 4:4 + span_x]
        neighbours = neighbours + padded[4:4 + depth_count, 4 - offset:4 - offset + span_y, 4:4 + span_x]
        neighbours = neighbours + padded[4:4 + depth_count, 4:4 + span_y, 4 + offset:4 + offset + span_x]
        neighbours = neighbours + padded[4:4 + depth_count, 4:4 + span_y, 4 - offset:4 - offset + span_x]
        summed = summed + COEFFS[offset] * neighbours
    return summed


def reference(fwd_prev, fwd_cur, adj_late, adj_now, courant, wavelet, boxes, sources, slab_top):
    cells_y = jnp.arange(NY).astype(jnp.int32)
    cells_x = jnp.arange(NX).astype(jnp.int32)
    cells_z = jnp.arange(NZ).astype(jnp.int32)

    def one_shot(shot_index):
        shot_box = boxes[shot_index]
        shot_source = sources[shot_index]
        inside_y = ((cells_y >= shot_box[0]) & (cells_y < shot_box[1])).astype(jnp.float32)
        inside_x = ((cells_x >= shot_box[2]) & (cells_x < shot_box[3])).astype(jnp.float32)
        box_mask = (inside_y[:, None] * inside_x[None, :])[None, :, :]
        spike_field = ((cells_z == shot_source[0])[:, None, None] & (cells_y == shot_source[1])[None, :, None]
                       & (cells_x == shot_source[2])[None, None, :]).astype(jnp.float32)
        field_zero = fwd_prev[shot_index]
        field_one = fwd_cur[shot_index]
        field_two = box_mask * (2.0 * field_one - field_zero + courant * laplace(field_one)
                                + wavelet[shot_index, 0] * spike_field)
        field_three = box_mask * (2.0 * field_two - field_one + courant * laplace(field_two)
                                  + wavelet[shot_index, 1] * spike_field)
        adj_three = adj_late[shot_index]
        adj_two = adj_now[shot_index]
        adj_one = box_mask * (2.0 * adj_two - adj_three + courant * laplace(adj_two))
        adj_zero = box_mask * (2.0 * adj_one - adj_two + courant * laplace(adj_one))
        image_cell = (adj_zero * (field_two - 2.0 * field_one + field_zero)
                      + adj_one * (field_three - 2.0 * field_two + field_one))
        return image_cell.reshape(NZ // 2, 2, NY // 2, 2, NX // 2, 2).mean(axis=(1, 3, 5))

    coarse_all = lax.map(one_shot, jnp.arange(SHOTS).astype(jnp.int32))
    summed = jnp.sum(coarse_all, axis=0)
    depth_index = slab_top[0].astype(jnp.float32) + 2.0 * jnp.arange(NZ // 2).astype(jnp.float32) + 1.0
    return summed * (0.25 + depth_index / 128.0)[:, None, None]
```

```python
import functools

import jax
import jax.numpy as jnp
from jax import lax
from jax.experimental import pallas as pl
from jax.experimental.pallas import tpu as pltpu
from jax.sharding import PartitionSpec as P

COEFFS = (-205.0 / 72.0, 8.0 / 5.0, -1.0 / 5.0, 8.0 / 315.0, -1.0 / 560.0)
MESH = pl.DeviceIdType.MESH
PAD = 8
LANES = 128


def kernel(
    shots, counts, wave_ref, box_ref, src_ref, top_ref, f0_hbm, f1_hbm, a3_hbm, a2_hbm, c_hbm, out_ref,
    now, mid, old, speed, image, strips_out, strips_in, merged, coarse, arrived,
    load_sem, send_sem, recv_sem, shot_send, shot_recv,
):
    county, countx = counts
    nz, ny = speed.shape[0], speed.shape[1]
    half, quarter = ny // 2, ny // 4
    planes = [(f, z) for f in range(2) for z in range(nz)]
    gy, gx, shot = lax.axis_index("gy"), lax.axis_index("gx"), lax.axis_index("shot")
    has_up, has_down = gy > 0, gy < county - 1
    has_left, has_right = gx > 0, gx < countx - 1

    loads = [
        pltpu.make_async_copy(f1_hbm.at[0], now.at[0, :, pl.ds(PAD, ny), :], load_sem.at[0]),
        pltpu.make_async_copy(a2_hbm.at[0], now.at[1, :, pl.ds(PAD, ny), :], load_sem.at[1]),
        pltpu.make_async_copy(c_hbm, speed, load_sem.at[2]),
        pltpu.make_async_copy(f0_hbm.at[0], old.at[0], load_sem.at[3]),
        pltpu.make_async_copy(a3_hbm.at[0], old.at[1], load_sem.at[4]),
    ]
    for load in loads:
        load.start()

    barrier = pltpu.get_barrier_semaphore()
    sides = [
        (has_up, {"gy": gy - 1}),
        (has_down, {"gy": gy + 1}),
        (has_left, {"gx": gx - 1}),
        (has_right, {"gx": gx + 1}),
    ]
    for there, device in sides:
        @pl.when(there)
        def _(device=device):
            pl.semaphore_signal(barrier, inc=1, device_id=device, device_id_type=MESH)
    for step in range(1, shots):
        pl.semaphore_signal(
            barrier, inc=1, device_id={"shot": lax.rem(shot + step, shots)}, device_id_type=MESH
        )
    expected = shots - 1
    for there, _ in sides:
        expected = expected + there.astype(jnp.int32)

    nothing = jnp.zeros((2, nz, PAD, LANES), jnp.float32)
    for there, start in ((has_up, 0), (has_down, PAD + ny)):
        @pl.when(jnp.logical_not(there))
        def _(start=start):
            now[:, :, pl.ds(start, PAD), :] = nothing
            mid[:, :, pl.ds(start, PAD), :] = nothing
    for there, side in ((has_left, 0), (has_right, 1)):
        @pl.when(jnp.logical_not(there))
        def _(side=side):
            strips_in[:, side] = jnp.zeros((2, quarter, LANES), jnp.float32)

    lane = lax.broadcasted_iota(jnp.int32, (8, LANES), 1)
    row = lax.broadcasted_iota(jnp.int32, (8, LANES), 0)
    group = lane // 8
    low = lax.rem(lane, 8) < 4

    def exchange(cells, phase):
        def remote(index, src, dst, device):
            return pltpu.make_async_remote_copy(
                src_ref=src, dst_ref=dst,
                send_sem=send_sem.at[phase, index], recv_sem=recv_sem.at[phase, index],
                device_id=device, device_id_type=MESH,
            )

        first, last = pl.ds(PAD, PAD), pl.ds(ny, PAD)
        above, below = pl.ds(0, PAD), pl.ds(PAD + ny, PAD)
        copies = [
            remote(0, cells.at[:, :, last, :], cells.at[:, :, above, :], {"gy": gy + 1}),
            remote(1, cells.at[:, :, first, :], cells.at[:, :, below, :], {"gy": gy - 1}),
            remote(2, strips_out.at[phase, 0], strips_in.at[phase, 0], {"gx": gx + 1}),
            remote(3, strips_out.at[phase, 1], strips_in.at[phase, 1], {"gx": gx - 1}),
        ]
        to = (has_down, has_up, has_right, has_left)
        came = (has_up, has_down, has_left, has_right)

        def start(which):
            for i in which:
                @pl.when(to[i])
                def _(i=i):
                    copies[i].start()

        def pack(i, carry):
            both = []
            for part in range(2):
                packed = jnp.zeros((8, LANES), jnp.float32)
                for q in range(2):
                    at = pl.multiple_of(i * 8, 8) + PAD + q * half + part * quarter
                    for p, (f, z) in enumerate(planes):
                        base = q * 64 + p * 8
                        moved = pltpu.roll(cells[f, z, pl.ds(at, 8), :], (base + 4) % LANES, 1)
                        packed = jnp.where(group == base // 8, moved, packed)
                both.append(packed)
            rows = pl.ds(pl.multiple_of(i * 8, 8), 8)
            strips_out[phase, 0, rows, :] = jnp.where(low, both[0], pltpu.roll(both[1], 4, 1))
            strips_out[phase, 1, rows, :] = jnp.where(
                low, pltpu.roll(both[0], LANES - 4, 1), both[1]
            )
            return carry

        def merge(i, carry):
            rows = pl.ds(pl.multiple_of(i * 8, 8), 8)
            left, right = strips_in[phase, 0, rows, :], strips_in[phase, 1, rows, :]
            merged[rows, :] = jnp.where(low, left, pltpu.roll(right, 4, 1))
            later = pl.ds(pl.multiple_of(i * 8 + quarter, 8), 8)
            merged[later, :] = jnp.where(low, pltpu.roll(left, LANES - 4, 1), right)
            return carry

        def finish():
            for i in range(4):
                @pl.when(to[i])
                def _(i=i):
                    copies[i].wait_send()
                @pl.when(came[i])
                def _(i=i):
                    copies[i].wait_recv()
            lax.fori_loop(0, quarter // 8, merge, 0)

        return start, pack, finish

    def laplacian(cells, f, at, q, halo):
        centre = [cells[f, z, pl.ds(at + PAD, 8), :] for z in range(nz)]
        result = []
        for z in range(nz):
            u = centre[z]
            base = q * 64 + (f * nz + z) * 8
            h = pltpu.roll(halo, (124 - base) % LANES, 1)
            total = (3.0 * COEFFS[0]) * u
            for k in range(1, 5):
                s = cells[f, z, pl.ds(at + (PAD + k), 8), :] + cells[f, z, pl.ds(at + (PAD - k), 8), :]
                s = s + pltpu.roll(jnp.where(lane < k, h, u), LANES - k, 1)
                s = s + pltpu.roll(jnp.where(lane >= LANES - k, h, u), k, 1)
                if z + k < nz:
                    s = s + centre[z + k]
                if z - k >= 0:
                    s = s + centre[z - k]
                total = total + COEFFS[k] * s
            result.append(total)
        return centre, result

    y0, y1, x0, x1 = box_ref[0, 0], box_ref[0, 1], box_ref[0, 2], box_ref[0, 3]
    sz, sy, sx = src_ref[0, 0], src_ref[0, 1], src_ref[0, 2]
    cell_x = gx * LANES + lane
    inside_x = (cell_x >= x0) & (cell_x < x1)
    source_x = cell_x == sx

    def place(at):
        cell_y = gy * ny + at + row
        inside = inside_x & (cell_y >= y0) & (cell_y < y1)
        return inside, source_x & (cell_y == sy)

    def amplitude(step, z):
        return jnp.where(sz == z, wave_ref[0, step], 0.0)

    def first_step(i, carry):
        halo = merged[pl.ds(pl.multiple_of(i * 8, 8), 8), :]
        for q in range(2):
            at = pl.multiple_of(i * 8 + q * half, 8)
            inside, source = place(at)
            for f in range(2):
                centre, lap = laplacian(now, f, at, q, halo)
                for z in range(nz):
                    new = 2.0 * centre[z] - old[f, z, pl.ds(at, 8), :]
                    new = new + speed[z, pl.ds(at, 8), :] * lap[z]
                    if f == 0:
                        new = new + jnp.where(source, amplitude(0, z), 0.0)
                    mid[f, z, pl.ds(at + PAD, 8), :] = jnp.where(inside, new, 0.0)
        return carry

    def second_step(i, carry):
        halo = merged[pl.ds(pl.multiple_of(i * 8, 8), 8), :]
        for q in range(2):
            at = pl.multiple_of(i * 8 + q * half, 8)
            inside, source = place(at)
            f2, lap_f = laplacian(mid, 0, at, q, halo)
            a1, lap_a = laplacian(mid, 1, at, q, halo)
            total = None
            for z in range(nz):
                c = speed[z, pl.ds(at, 8), :]
                f0 = old[0, z, pl.ds(at, 8), :]
                f1 = now[0, z, pl.ds(at + PAD, 8), :]
                a2 = now[1, z, pl.ds(at + PAD, 8), :]
                bent = f2[z] - 2.0 * f1
                f3 = 2.0 * f2[z] - f1 + c * lap_f[z] + jnp.where(source, amplitude(1, z), 0.0)
                f3 = jnp.where(inside, f3, 0.0)
                a0 = jnp.where(inside, 2.0 * a1[z] - a2 + c * lap_a[z], 0.0)
                part = a0 * (bent + f0) + a1[z] * (f3 - 2.0 * f2[z] + f1)
                total = part if z % 2 == 0 else total + part
                if z % 2 == 1:
                    image[z // 2, pl.ds(at, 8), :] = total
        return carry

    loads[0].wait()
    loads[1].wait()
    pl.semaphore_wait(barrier, expected)
    start, pack, finish = exchange(now, 0)
    start((0, 1))
    lax.fori_loop(0, quarter // 8, pack, 0)
    start((2, 3))
    for load in loads[2:]:
        load.wait()
    finish()
    lax.fori_loop(0, half // 8, first_step, 0)

    start, pack, finish = exchange(mid, 1)
    start((0, 1))
    lax.fori_loop(0, quarter // 8, pack, 0)
    start((2, 3))
    finish()
    lax.fori_loop(0, half // 8, second_step, 0)

    pair = lax.broadcasted_iota(jnp.int32, (LANES, LANES), 0) // 2
    column = lax.broadcasted_iota(jnp.int32, (LANES, LANES), 1)
    total = None
    for k in range(nz // 2):
        rows = image[k, pl.ds(0, half, stride=2), :] + image[k, pl.ds(1, half, stride=2), :]
        pick = (column == pair + 64 * k).astype(jnp.float32)
        part = jnp.dot(rows, pick, precision=lax.Precision.HIGHEST, preferred_element_type=jnp.float32)
        total = part if total is None else total + part
    coarse[...] = total
    sends = []
    for step in range(1, shots):
        copy = pltpu.make_async_remote_copy(
            src_ref=coarse, dst_ref=arrived.at[step - 1],
            send_sem=shot_send.at[step - 1], recv_sem=shot_recv.at[step - 1],
            device_id={"shot": lax.rem(shot + step, shots)}, device_id_type=MESH,
        )
        copy.start()
        sends.append(copy)
    for step, copy in enumerate(sends):
        copy.wait_recv()
        total = total + arrived[step]
    depth = top_ref[0].astype(jnp.float32)
    for k in range(nz // 2):
        factor = (0.25 + (depth + (2.0 * k + 1.0)) / 128.0) * 0.125
        out_ref[k] = total[:, 64 * k : 64 * k + 64] * factor
    for copy in sends:
        copy.wait_send()


def per_device(shots, counts, fwd_prev, fwd_cur, adj_late, adj_now, courant, wavelet, boxes, sources, slab_top):
    nz, ny, nx = courant.shape
    f32 = jnp.float32
    smem = pl.BlockSpec(memory_space=pltpu.SMEM)
    hbm = pl.BlockSpec(memory_space=pl.ANY)
    return pl.pallas_call(
        functools.partial(kernel, shots, counts),
        out_shape=jax.ShapeDtypeStruct((nz // 2, ny // 2, nx // 2), f32),
        in_specs=[smem] * 4 + [hbm] * 5,
        out_specs=pl.BlockSpec(memory_space=pltpu.VMEM),
        scratch_shapes=[
            pltpu.VMEM((2, nz, ny + 2 * PAD, nx), f32),
            pltpu.VMEM((2, nz, ny + 2 * PAD, nx), f32),
            pltpu.VMEM((2, nz, ny, nx), f32),
            pltpu.VMEM((nz, ny, nx), f32),
            pltpu.VMEM((nz // 2, ny, nx), f32),
            pltpu.VMEM((2, 2, ny // 4, nx), f32),
            pltpu.VMEM((2, 2, ny // 4, nx), f32),
            pltpu.VMEM((ny // 2, nx), f32),
            pltpu.VMEM((ny // 2, nx), f32),
            pltpu.VMEM((max(shots - 1, 1), ny // 2, nx), f32),
            pltpu.SemaphoreType.DMA((5,)),
            pltpu.SemaphoreType.DMA((2, 4)),
            pltpu.SemaphoreType.DMA((2, 4)),
            pltpu.SemaphoreType.DMA((max(shots - 1, 1),)),
            pltpu.SemaphoreType.DMA((max(shots - 1, 1),)),
        ],
        compiler_params=pltpu.CompilerParams(
            collective_id=0, has_side_effects=True, vmem_limit_bytes=32 * 1024 * 1024
        ),
    )(wavelet, boxes, sources, slab_top, fwd_prev, fwd_cur, adj_late, adj_now, courant)


def solution(mesh):
    shots = mesh.shape["shot"]
    counts = (mesh.shape["gy"], mesh.shape["gx"])
    return jax.shard_map(
        functools.partial(per_device, shots, counts),
        mesh=mesh,
        in_specs=(
            P("shot", None, "gy", "gx"),
            P("shot", None, "gy", "gx"),
            P("shot", None, "gy", "gx"),
            P("shot", None, "gy", "gx"),
            P(None, "gy", "gx"),
            P("shot", None),
            P("shot", None),
            P("shot", None),
            P(),
        ),
        out_specs=P(None, "gy", "gx"),
        check_vma=False,
    )
```

```python
import functools

import jax
import jax.numpy as jnp
from jax import lax
from jax.experimental import pallas as pl
from jax.experimental.pallas import tpu as pltpu
from jax.sharding import PartitionSpec as P

COEFFS = (-205.0 / 72.0, 8.0 / 5.0, -1.0 / 5.0, 8.0 / 315.0, -1.0 / 560.0)
MESH = pl.DeviceIdType.MESH
PAD = 8
LANES = 128
ROWS = 16


def kernel(
    shots, counts, wave_ref, box_ref, src_ref, top_ref, f0_hbm, f1_hbm, a3_hbm, a2_hbm, c_hbm, out_ref,
    now, mid, old, speed, image, strips_out, strips_in, own, fix, ring, band, coarse, arrived,
    load_sem, send_sem, recv_sem, shot_send, shot_recv,
):
    county, countx = counts
    nz, ny = speed.shape[0], speed.shape[1]
    half, quarter = ny // 2, ny // 4
    planes = [(f, z) for f in range(2) for z in range(nz)]
    gy, gx, shot = lax.axis_index("gy"), lax.axis_index("gx"), lax.axis_index("shot")
    has_up, has_down = gy > 0, gy < county - 1
    has_left, has_right = gx > 0, gx < countx - 1

    loads = [
        pltpu.make_async_copy(f1_hbm.at[0], now.at[0, :, pl.ds(PAD, ny), :], load_sem.at[0]),
        pltpu.make_async_copy(a2_hbm.at[0], now.at[1, :, pl.ds(PAD, ny), :], load_sem.at[1]),
        pltpu.make_async_copy(c_hbm, speed, load_sem.at[2]),
        pltpu.make_async_copy(f0_hbm.at[0], old.at[0], load_sem.at[3]),
        pltpu.make_async_copy(a3_hbm.at[0], old.at[1], load_sem.at[4]),
    ]
    for load in loads:
        load.start()

    barrier = pltpu.get_barrier_semaphore()
    sides = [
        (has_up, {"gy": gy - 1}),
        (has_down, {"gy": gy + 1}),
        (has_left, {"gx": gx - 1}),
        (has_right, {"gx": gx + 1}),
    ]
    for there, device in sides:
        @pl.when(there)
        def _(device=device):
            pl.semaphore_signal(barrier, inc=1, device_id=device, device_id_type=MESH)
    for step in range(1, shots):
        pl.semaphore_signal(
            barrier, inc=1, device_id={"shot": lax.rem(shot + step, shots)}, device_id_type=MESH
        )
    expected = shots - 1
    for there, _ in sides:
        expected = expected + there.astype(jnp.int32)

    nothing = jnp.zeros((2, nz, PAD, LANES), jnp.float32)
    for there, start in ((has_up, 0), (has_down, PAD + ny)):
        @pl.when(jnp.logical_not(there))
        def _(start=start):
            now[:, :, pl.ds(start, PAD), :] = nothing
            mid[:, :, pl.ds(start, PAD), :] = nothing
    for there, side in ((has_left, 0), (has_right, 1)):
        @pl.when(jnp.logical_not(there))
        def _(side=side):
            strips_in[:, side] = jnp.zeros((2, quarter, LANES), jnp.float32)

    lane = lax.broadcasted_iota(jnp.int32, (8, LANES), 1)
    group = lane // 8
    low = lax.rem(lane, 8) < 4
    edge = (lane < 4) | (lane >= LANES - 4)

    ri = lax.broadcasted_iota(jnp.int32, (LANES, LANES), 0)
    ci = lax.broadcasted_iota(jnp.int32, (LANES, LANES), 1)
    apart = jnp.abs(ri - ci)
    around = jnp.minimum(apart, LANES - apart)
    crossing = (ri // 8 == ci // 8) & ((lax.rem(ri, 8) < 4) != (lax.rem(ci, 8) < 4))
    weights = jnp.zeros((LANES, LANES), jnp.float32)
    crossed = weights
    for k in range(1, 5):
        weights = jnp.where(around == k, COEFFS[k], weights)
        crossed = jnp.where(crossing & (apart == k), COEFFS[k], crossed)
    for ref, whole in ((ring, weights), (band, crossed)):
        high = whole.astype(jnp.bfloat16)
        ref[0:LANES] = high
        ref[LANES : 2 * LANES] = high
        ref[2 * LANES : 3 * LANES] = (whole - high.astype(jnp.float32)).astype(jnp.bfloat16)

    def times(x, ref):
        high = x.astype(jnp.bfloat16)
        rest = (x - high.astype(jnp.float32)).astype(jnp.bfloat16)
        return jnp.dot(
            jnp.concatenate([high, rest, high], 1), ref[...], preferred_element_type=jnp.float32
        )

    def stencil(cells, at):
        centre = [cells[f, z, pl.ds(at + PAD, ROWS), :] for f, z in planes]
        along_x = times(jnp.concatenate(centre, 0), ring)
        result = []
        for p, (f, z) in enumerate(planes):
            total = along_x[p * ROWS : (p + 1) * ROWS] + (3.0 * COEFFS[0]) * centre[p]
            for k in range(1, 5):
                s = cells[f, z, pl.ds(at + (PAD + k), ROWS), :]
                s = s + cells[f, z, pl.ds(at + (PAD - k), ROWS), :]
                if z + k < nz:
                    s = s + centre[p + k]
                if z - k >= 0:
                    s = s + centre[p - k]
                total = total + COEFFS[k] * s
            result.append(total)
        return centre, result

    y0, y1, x0, x1 = box_ref[0, 0], box_ref[0, 1], box_ref[0, 2], box_ref[0, 3]
    sz, sy, sx = src_ref[0, 0], src_ref[0, 1], src_ref[0, 2]

    def place(at, rows):
        cell_y = gy * ny + at + lax.broadcasted_iota(jnp.int32, (rows, LANES), 0)
        cell_x = gx * LANES + lax.broadcasted_iota(jnp.int32, (rows, LANES), 1)
        inside = (cell_x >= x0) & (cell_x < x1) & (cell_y >= y0) & (cell_y < y1)
        return inside, (cell_x == sx) & (cell_y == sy)

    def amplitude(step, z):
        return jnp.where(sz == z, wave_ref[0, step], 0.0)

    def first_step(i, carry):
        at = pl.multiple_of(i * ROWS, ROWS)
        here = pl.ds(at, ROWS)
        inside, source = place(at, ROWS)
        centre, lap = stencil(now, at)
        for p, (f, z) in enumerate(planes):
            new = 2.0 * centre[p] - old[f, z, here, :] + speed[z, here, :] * lap[p]
            if f == 0:
                new = new + jnp.where(source, amplitude(0, z), 0.0)
            mid[f, z, pl.ds(at + PAD, ROWS), :] = jnp.where(inside, new, 0.0)
        return carry

    def second_step(i, carry):
        at = pl.multiple_of(i * ROWS, ROWS)
        here, padded = pl.ds(at, ROWS), pl.ds(at + PAD, ROWS)
        inside, source = place(at, ROWS)
        centre, lap = stencil(mid, at)
        total = None
        for z in range(nz):
            c = speed[z, here, :]
            f0, f1, a2 = old[0, z, here, :], now[0, z, padded, :], now[1, z, padded, :]
            f2, a1 = centre[z], centre[nz + z]
            f3 = 2.0 * f2 - f1 + c * lap[z] + jnp.where(source, amplitude(1, z), 0.0)
            f3 = jnp.where(inside, f3, 0.0)
            a0 = jnp.where(inside, 2.0 * a1 - a2 + c * lap[nz + z], 0.0)
            part = a0 * (f2 - 2.0 * f1 + f0) + a1 * (f3 - 2.0 * f2 + f1)
            total = part if z % 2 == 0 else total + part
            if z % 2 == 1:
                image[z // 2, here, :] = total
        return carry

    def spot(i, part, q):
        return pl.multiple_of(i * 8, 8) + (q * half + part * quarter)

    def packing(phase, value):
        def pack(i, carry):
            both = []
            for part in range(2):
                packed = jnp.zeros((8, LANES), jnp.float32)
                for q in range(2):
                    for p, cells in enumerate(value(i, part, q)):
                        base = q * 64 + p * 8
                        moved = pltpu.roll(cells, (base + 4) % LANES, 1)
                        packed = jnp.where(group == base // 8, moved, packed)
                own[pl.ds(pl.multiple_of(i * 8, 8) + part * quarter, 8), :] = packed
                both.append(packed)
            rows = pl.ds(pl.multiple_of(i * 8, 8), 8)
            strips_out[phase, 0, rows, :] = jnp.where(low, both[0], pltpu.roll(both[1], 4, 1))
            strips_out[phase, 1, rows, :] = jnp.where(
                low, pltpu.roll(both[0], LANES - 4, 1), both[1]
            )
            return carry

        lax.fori_loop(0, quarter // 8, pack, 0, unroll=2)

    def plain(i, part, q):
        return [now[f, z, pl.ds(spot(i, part, q) + PAD, 8), :] for f, z in planes]

    def fixes(i, part, q):
        packed = fix[pl.ds(pl.multiple_of(i * 8, 8) + part * quarter, 8), :]
        at = spot(i, part, q)
        inside, _ = place(at, 8)
        result = []
        for p, (f, z) in enumerate(planes):
            moved = pltpu.roll(packed, (124 - q * 64 - p * 8) % LANES, 1)
            result.append(jnp.where(inside & edge, speed[z, pl.ds(at, 8), :] * moved, 0.0))
        return result

    def fixed_middle(i, part, q):
        padded = pl.ds(spot(i, part, q) + PAD, 8)
        result = []
        for (f, z), lack in zip(planes, fixes(i, part, q)):
            value = mid[f, z, padded, :] + lack
            mid[f, z, padded, :] = value
            result.append(value)
        return result

    def fix_image(i, carry):
        for part in range(2):
            for q in range(2):
                at = spot(i, part, q)
                here, padded = pl.ds(at, 8), pl.ds(at + PAD, 8)
                lack = fixes(i, part, q)
                for z in range(0, nz, 2):
                    total = image[z // 2, here, :]
                    for d in (z, z + 1):
                        bent = mid[0, d, padded, :] - 2.0 * now[0, d, padded, :] + old[0, d, here, :]
                        total = total + lack[nz + d] * bent + mid[1, d, padded, :] * lack[d]
                    image[z // 2, here, :] = total
        return carry

    to = (has_down, has_up, has_right, has_left)
    came = (has_up, has_down, has_left, has_right)

    def exchange(cells, phase):
        def remote(index, src, dst, device):
            return pltpu.make_async_remote_copy(
                src_ref=src, dst_ref=dst,
                send_sem=send_sem.at[phase, index], recv_sem=recv_sem.at[phase, index],
                device_id=device, device_id_type=MESH,
            )

        first, last = pl.ds(PAD, PAD), pl.ds(ny, PAD)
        above, below = pl.ds(0, PAD), pl.ds(PAD + ny, PAD)
        return [
            remote(0, cells.at[:, :, last, :], cells.at[:, :, above, :], {"gy": gy + 1}),
            remote(1, cells.at[:, :, first, :], cells.at[:, :, below, :], {"gy": gy - 1}),
            remote(2, strips_out.at[phase, 0], strips_in.at[phase, 0], {"gx": gx + 1}),
            remote(3, strips_out.at[phase, 1], strips_in.at[phase, 1], {"gx": gx - 1}),
        ]

    def when(conditions, copies, action, which):
        for i in which:
            @pl.when(conditions[i])
            def _(i=i):
                getattr(copies[i], action)()

    def merge(phase):
        left, right = strips_in[phase, 0], strips_in[phase, 1]
        few = lax.rem(lax.broadcasted_iota(jnp.int32, (quarter, LANES), 1), 8) < 4
        both = jnp.concatenate(
            [
                jnp.where(few, left, pltpu.roll(right, 4, 1)),
                jnp.where(few, pltpu.roll(left, LANES - 4, 1), right),
            ],
            0,
        )
        fix[...] = times(both - own[...], band)

    chunks = ny // ROWS
    border = chunks - 1
    loads[0].wait()
    loads[1].wait()
    pl.semaphore_wait(barrier, expected)
    early = exchange(now, 0)
    when(to, early, "start", (0, 1))
    packing(0, plain)
    when(to, early, "start", (2, 3))
    for load in loads[2:]:
        load.wait()
    lax.fori_loop(1, border, first_step, 0)
    when(came, early, "wait_recv", (0, 1))
    lax.fori_loop(0, 2, lambda i, carry: first_step(i * border, carry), 0)
    when(came, early, "wait_recv", (2, 3))
    merge(0)
    packing(1, fixed_middle)

    late = exchange(mid, 1)
    when(to, late, "start", (2, 3, 0, 1))
    lax.fori_loop(1, border, second_step, 0)
    when(came, late, "wait_recv", (0, 1))
    lax.fori_loop(0, 2, lambda i, carry: second_step(i * border, carry), 0)
    when(came, late, "wait_recv", (2, 3))
    merge(1)
    lax.fori_loop(0, quarter // 8, fix_image, 0)

    pair = lax.broadcasted_iota(jnp.int32, (LANES, LANES), 0) // 2
    column = lax.broadcasted_iota(jnp.int32, (LANES, LANES), 1)
    total = None
    for k in range(nz // 2):
        rows = image[k, pl.ds(0, half, stride=2), :] + image[k, pl.ds(1, half, stride=2), :]
        pick = (column == pair + 64 * k).astype(jnp.float32)
        part = jnp.dot(rows, pick, precision=lax.Precision.HIGHEST, preferred_element_type=jnp.float32)
        total = part if total is None else total + part
    coarse[...] = total
    sends = []
    for step in range(1, shots):
        copy = pltpu.make_async_remote_copy(
            src_ref=coarse, dst_ref=arrived.at[step - 1],
            send_sem=shot_send.at[step - 1], recv_sem=shot_recv.at[step - 1],
            device_id={"shot": lax.rem(shot + step, shots)}, device_id_type=MESH,
        )
        copy.start()
        sends.append(copy)
    for step, copy in enumerate(sends):
        copy.wait_recv()
        total = total + arrived[step]
    depth = top_ref[0].astype(jnp.float32)
    for k in range(nz // 2):
        factor = (0.25 + (depth + (2.0 * k + 1.0)) / 128.0) * 0.125
        out_ref[k] = total[:, 64 * k : 64 * k + 64] * factor
    for copy in sends:
        copy.wait_send()
    when(to, early, "wait_send", range(4))
    when(to, late, "wait_send", range(4))


def per_device(shots, counts, fwd_prev, fwd_cur, adj_late, adj_now, courant, wavelet, boxes, sources, slab_top):
    nz, ny, nx = courant.shape
    f32 = jnp.float32
    smem = pl.BlockSpec(memory_space=pltpu.SMEM)
    hbm = pl.BlockSpec(memory_space=pltpu.HBM)
    return pl.pallas_call(
        functools.partial(kernel, shots, counts),
        out_shape=jax.ShapeDtypeStruct((nz // 2, ny // 2, nx // 2), f32),
        in_specs=[smem] * 4 + [hbm] * 5,
        out_specs=pl.BlockSpec(memory_space=pltpu.VMEM),
        scratch_shapes=[
            pltpu.VMEM((2, nz, ny + 2 * PAD, nx), f32),
            pltpu.VMEM((2, nz, ny + 2 * PAD, nx), f32),
            pltpu.VMEM((2, nz, ny, nx), f32),
            pltpu.VMEM((nz, ny, nx), f32),
            pltpu.VMEM((nz // 2, ny, nx), f32),
            pltpu.VMEM((2, 2, ny // 4, nx), f32),
            pltpu.VMEM((2, 2, ny // 4, nx), f32),
            pltpu.VMEM((ny // 2, nx), f32),
            pltpu.VMEM((ny // 2, nx), f32),
            pltpu.VMEM((3 * nx, nx), jnp.bfloat16),
            pltpu.VMEM((3 * nx, nx), jnp.bfloat16),
            pltpu.VMEM((ny // 2, nx), f32),
            pltpu.VMEM((max(shots - 1, 1), ny // 2, nx), f32),
            pltpu.SemaphoreType.DMA((5,)),
            pltpu.SemaphoreType.DMA((2, 4)),
            pltpu.SemaphoreType.DMA((2, 4)),
            pltpu.SemaphoreType.DMA((max(shots - 1, 1),)),
            pltpu.SemaphoreType.DMA((max(shots - 1, 1),)),
        ],
        compiler_params=pltpu.CompilerParams(
            collective_id=0, has_side_effects=True, vmem_limit_bytes=56 * 1024 * 1024
        ),
    )(wavelet, boxes, sources, slab_top, fwd_prev, fwd_cur, adj_late, adj_now, courant)


def solution(mesh):
    shots = mesh.shape["shot"]
    counts = (mesh.shape["gy"], mesh.shape["gx"])
    return jax.shard_map(
        functools.partial(per_device, shots, counts),
        mesh=mesh,
        in_specs=(
            P("shot", None, "gy", "gx"),
            P("shot", None, "gy", "gx"),
            P("shot", None, "gy", "gx"),
            P("shot", None, "gy", "gx"),
            P(None, "gy", "gx"),
            P("shot", None),
            P("shot", None),
            P("shot", None),
            P(),
        ),
        out_specs=P(None, "gy", "gx"),
        check_vma=False,
    )
```

```python
import functools

import jax
import jax.numpy as jnp
from jax import lax
from jax.experimental import pallas as pl
from jax.experimental.pallas import tpu as pltpu
from jax.sharding import PartitionSpec as P

COEFFS = (-205.0 / 72.0, 8.0 / 5.0, -1.0 / 5.0, 8.0 / 315.0, -1.0 / 560.0)
MESH = pl.DeviceIdType.MESH
PAD = 8
LANES = 128
ROWS = 16


def kernel(
    shots, counts, wave_ref, box_ref, src_ref, top_ref, f0_hbm, f1_hbm, a3_hbm, a2_hbm, c_hbm, out_ref,
    now, mid, old, speed, image, strips_out, strips_in, own, fix, ring, band, coarse, arrived,
    load_sem, send_sem, recv_sem, shot_send, shot_recv,
):
    county, countx = counts
    nz, ny = speed.shape[0], speed.shape[1]
    half, quarter = ny // 2, ny // 4
    planes = [(f, z) for f in range(2) for z in range(nz)]
    gy, gx, shot = lax.axis_index("gy"), lax.axis_index("gx"), lax.axis_index("shot")
    has_up, has_down = gy > 0, gy < county - 1
    has_left, has_right = gx > 0, gx < countx - 1

    loads = [
        pltpu.make_async_copy(f1_hbm.at[0], now.at[0, :, pl.ds(PAD, ny), :], load_sem.at[0]),
        pltpu.make_async_copy(a2_hbm.at[0], now.at[1, :, pl.ds(PAD, ny), :], load_sem.at[1]),
        pltpu.make_async_copy(c_hbm, speed, load_sem.at[2]),
        pltpu.make_async_copy(f0_hbm.at[0], old.at[0], load_sem.at[3]),
        pltpu.make_async_copy(a3_hbm.at[0], old.at[1], load_sem.at[4]),
    ]
    for load in loads:
        load.start()

    barrier = pltpu.get_barrier_semaphore()
    sides = [
        (has_up, {"gy": gy - 1}),
        (has_down, {"gy": gy + 1}),
        (has_left, {"gx": gx - 1}),
        (has_right, {"gx": gx + 1}),
    ]
    for there, device in sides:
        @pl.when(there)
        def _(device=device):
            pl.semaphore_signal(barrier, inc=1, device_id=device, device_id_type=MESH)
    for step in range(1, shots):
        pl.semaphore_signal(
            barrier, inc=1, device_id={"shot": lax.rem(shot + step, shots)}, device_id_type=MESH
        )
    expected = shots - 1
    for there, _ in sides:
        expected = expected + there.astype(jnp.int32)

    nothing = jnp.zeros((2, nz, PAD, LANES), jnp.float32)
    for there, start in ((has_up, 0), (has_down, PAD + ny)):
        @pl.when(jnp.logical_not(there))
        def _(start=start):
            now[:, :, pl.ds(start, PAD), :] = nothing
            mid[:, :, pl.ds(start, PAD), :] = nothing
    for there, side in ((has_left, 0), (has_right, 1)):
        @pl.when(jnp.logical_not(there))
        def _(side=side):
            strips_in[:, side] = jnp.zeros((2, quarter, LANES), jnp.float32)

    lane = lax.broadcasted_iota(jnp.int32, (8, LANES), 1)
    group = lane // 8
    low = lax.rem(lane, 8) < 4
    edge = (lane < 4) | (lane >= LANES - 4)

    ri = lax.broadcasted_iota(jnp.int32, (LANES, LANES), 0)
    ci = lax.broadcasted_iota(jnp.int32, (LANES, LANES), 1)
    apart = jnp.abs(ri - ci)
    around = jnp.minimum(apart, LANES - apart)
    crossing = (ri // 8 == ci // 8) & ((lax.rem(ri, 8) < 4) != (lax.rem(ci, 8) < 4))
    weights = jnp.zeros((LANES, LANES), jnp.float32)
    crossed = weights
    for k in range(1, 5):
        weights = jnp.where(around == k, COEFFS[k], weights)
        crossed = jnp.where(crossing & (apart == k), COEFFS[k], crossed)
    for ref, whole in ((ring, weights), (band, crossed)):
        high = whole.astype(jnp.bfloat16)
        ref[0:LANES] = high
        ref[LANES : 2 * LANES] = high
        ref[2 * LANES : 3 * LANES] = (whole - high.astype(jnp.float32)).astype(jnp.bfloat16)

    def times(x, ref):
        high = x.astype(jnp.bfloat16)
        rest = (x - high.astype(jnp.float32)).astype(jnp.bfloat16)
        return jnp.dot(
            jnp.concatenate([high, rest, high], 1), ref[...], preferred_element_type=jnp.float32
        )

    def stencil(cells, at):
        centre = [cells[f, z, pl.ds(at + PAD, ROWS), :] for f, z in planes]
        along_x = times(jnp.concatenate(centre, 0), ring)
        result = []
        for p, (f, z) in enumerate(planes):
            total = along_x[p * ROWS : (p + 1) * ROWS] + (3.0 * COEFFS[0]) * centre[p]
            for k in range(1, 5):
                s = cells[f, z, pl.ds(at + (PAD + k), ROWS), :]
                s = s + cells[f, z, pl.ds(at + (PAD - k), ROWS), :]
                if z + k < nz:
                    s = s + centre[p + k]
                if z - k >= 0:
                    s = s + centre[p - k]
                total = total + COEFFS[k] * s
            result.append(total)
        return centre, result

    y0, y1, x0, x1 = box_ref[0, 0], box_ref[0, 1], box_ref[0, 2], box_ref[0, 3]
    sz, sy, sx = src_ref[0, 0], src_ref[0, 1], src_ref[0, 2]

    def place(at, rows):
        cell_y = gy * ny + at + lax.broadcasted_iota(jnp.int32, (rows, LANES), 0)
        cell_x = gx * LANES + lax.broadcasted_iota(jnp.int32, (rows, LANES), 1)
        inside = (cell_x >= x0) & (cell_x < x1) & (cell_y >= y0) & (cell_y < y1)
        return inside, (cell_x == sx) & (cell_y == sy)

    def amplitude(step, z):
        return jnp.where(sz == z, wave_ref[0, step], 0.0)

    def first_step(i, carry):
        at = pl.multiple_of(i * ROWS, ROWS)
        here = pl.ds(at, ROWS)
        inside, source = place(at, ROWS)
        centre, lap = stencil(now, at)
        for p, (f, z) in enumerate(planes):
            new = 2.0 * centre[p] - old[f, z, here, :] + speed[z, here, :] * lap[p]
            if f == 0:
                new = new + jnp.where(source, amplitude(0, z), 0.0)
            mid[f, z, pl.ds(at + PAD, ROWS), :] = jnp.where(inside, new, 0.0)
        return carry

    def second_step(i, carry):
        at = pl.multiple_of(i * ROWS, ROWS)
        here, padded = pl.ds(at, ROWS), pl.ds(at + PAD, ROWS)
        inside, source = place(at, ROWS)
        centre, lap = stencil(mid, at)
        total = None
        for z in range(nz):
            c = speed[z, here, :]
            f0, f1, a2 = old[0, z, here, :], now[0, z, padded, :], now[1, z, padded, :]
            f2, a1 = centre[z], centre[nz + z]
            f3 = 2.0 * f2 - f1 + c * lap[z] + jnp.where(source, amplitude(1, z), 0.0)
            f3 = jnp.where(inside, f3, 0.0)
            a0 = jnp.where(inside, 2.0 * a1 - a2 + c * lap[nz + z], 0.0)
            part = a0 * (f2 - 2.0 * f1 + f0) + a1 * (f3 - 2.0 * f2 + f1)
            total = part if z % 2 == 0 else total + part
            if z % 2 == 1:
                image[z // 2, here, :] = total
        return carry

    def spot(i, part, q):
        return pl.multiple_of(i * 8, 8) + (q * half + part * quarter)

    def packing(phase, value):
        def pack(i, carry):
            both = []
            for part in range(2):
                packed = jnp.zeros((8, LANES), jnp.float32)
                for q in range(2):
                    for p, cells in enumerate(value(i, part, q)):
                        base = q * 64 + p * 8
                        moved = pltpu.roll(cells, (base + 4) % LANES, 1)
                        packed = jnp.where(group == base // 8, moved, packed)
                own[pl.ds(pl.multiple_of(i * 8, 8) + part * quarter, 8), :] = packed
                both.append(packed)
            rows = pl.ds(pl.multiple_of(i * 8, 8), 8)
            strips_out[phase, 0, rows, :] = jnp.where(low, both[0], pltpu.roll(both[1], 4, 1))
            strips_out[phase, 1, rows, :] = jnp.where(
                low, pltpu.roll(both[0], LANES - 4, 1), both[1]
            )
            return carry

        lax.fori_loop(0, quarter // 8, pack, 0, unroll=2)

    def plain(i, part, q):
        return [now[f, z, pl.ds(spot(i, part, q) + PAD, 8), :] for f, z in planes]

    def fixes(i, part, q):
        packed = fix[pl.ds(pl.multiple_of(i * 8, 8) + part * quarter, 8), :]
        at = spot(i, part, q)
        inside, _ = place(at, 8)
        result = []
        for p, (f, z) in enumerate(planes):
            moved = pltpu.roll(packed, (124 - q * 64 - p * 8) % LANES, 1)
            result.append(jnp.where(inside & edge, speed[z, pl.ds(at, 8), :] * moved, 0.0))
        return result

    def fixed_middle(i, part, q):
        padded = pl.ds(spot(i, part, q) + PAD, 8)
        result = []
        for (f, z), lack in zip(planes, fixes(i, part, q)):
            value = mid[f, z, padded, :] + lack
            mid[f, z, padded, :] = value
            result.append(value)
        return result

    def fix_image(i, carry):
        for part in range(2):
            for q in range(2):
                at = spot(i, part, q)
                here, padded = pl.ds(at, 8), pl.ds(at + PAD, 8)
                lack = fixes(i, part, q)
                for z in range(0, nz, 2):
                    total = image[z // 2, here, :]
                    for d in (z, z + 1):
                        bent = mid[0, d, padded, :] - 2.0 * now[0, d, padded, :] + old[0, d, here, :]
                        total = total + lack[nz + d] * bent + mid[1, d, padded, :] * lack[d]
                    image[z // 2, here, :] = total
        return carry

    to = (has_down, has_up, has_right, has_left)
    came = (has_up, has_down, has_left, has_right)

    def exchange(cells, phase):
        def remote(index, src, dst, device):
            return pltpu.make_async_remote_copy(
                src_ref=src, dst_ref=dst,
                send_sem=send_sem.at[phase, index], recv_sem=recv_sem.at[phase, index],
                device_id=device, device_id_type=MESH,
            )

        first, last = pl.ds(PAD, PAD), pl.ds(ny, PAD)
        above, below = pl.ds(0, PAD), pl.ds(PAD + ny, PAD)
        return [
            remote(0, cells.at[:, :, last, :], cells.at[:, :, above, :], {"gy": gy + 1}),
            remote(1, cells.at[:, :, first, :], cells.at[:, :, below, :], {"gy": gy - 1}),
            remote(2, strips_out.at[phase, 0], strips_in.at[phase, 0], {"gx": gx + 1}),
            remote(3, strips_out.at[phase, 1], strips_in.at[phase, 1], {"gx": gx - 1}),
        ]

    def when(conditions, copies, action, which):
        for i in which:
            @pl.when(conditions[i])
            def _(i=i):
                getattr(copies[i], action)()

    def merge(phase):
        left, right = strips_in[phase, 0], strips_in[phase, 1]
        few = lax.rem(lax.broadcasted_iota(jnp.int32, (quarter, LANES), 1), 8) < 4
        both = jnp.concatenate(
            [
                jnp.where(few, left, pltpu.roll(right, 4, 1)),
                jnp.where(few, pltpu.roll(left, LANES - 4, 1), right),
            ],
            0,
        )
        fix[...] = times(both - own[...], band)

    chunks = ny // ROWS
    border = chunks - 1
    loads[0].wait()
    loads[1].wait()
    pl.semaphore_wait(barrier, expected)
    early = exchange(now, 0)
    when(to, early, "start", (0, 1))
    packing(0, plain)
    when(to, early, "start", (2, 3))
    for load in loads[2:]:
        load.wait()
    lax.fori_loop(1, border, first_step, 0)
    when(came, early, "wait_recv", (0, 1))
    lax.fori_loop(0, 2, lambda i, carry: first_step(i * border, carry), 0)
    when(came, early, "wait_recv", (2, 3))
    merge(0)
    packing(1, fixed_middle)

    late = exchange(mid, 1)
    when(to, late, "start", (2, 3, 0, 1))
    lax.fori_loop(1, border, second_step, 0)
    when(came, late, "wait_recv", (0, 1))
    lax.fori_loop(0, 2, lambda i, carry: second_step(i * border, carry), 0)
    when(came, late, "wait_recv", (2, 3))
    merge(1)
    lax.fori_loop(0, quarter // 8, fix_image, 0)

    pair = lax.broadcasted_iota(jnp.int32, (LANES, LANES), 0) // 2
    column = lax.broadcasted_iota(jnp.int32, (LANES, LANES), 1)
    total = None
    for k in range(nz // 2):
        rows = image[k, pl.ds(0, half, stride=2), :] + image[k, pl.ds(1, half, stride=2), :]
        pick = (column == pair + 64 * k).astype(jnp.float32)
        part = lax.dot_general(
            pick, rows, (((0,), (1,)), ((), ())),
            precision=lax.Precision.HIGHEST, preferred_element_type=jnp.float32,
        )
        total = part if total is None else total + part
    coarse[...] = total
    sends = []
    for step in range(1, shots):
        copy = pltpu.make_async_remote_copy(
            src_ref=coarse, dst_ref=arrived.at[step - 1],
            send_sem=shot_send.at[step - 1], recv_sem=shot_recv.at[step - 1],
            device_id={"shot": lax.rem(shot + step, shots)}, device_id_type=MESH,
        )
        copy.start()
        sends.append(copy)
    for step, copy in enumerate(sends):
        copy.wait_recv()
        total = total + arrived[step]
    depth = top_ref[0].astype(jnp.float32)
    for k in range(nz // 2):
        factor = (0.25 + (depth + (2.0 * k + 1.0)) / 128.0) * 0.125
        out_ref[k] = total[64 * k : 64 * k + 64] * factor
    for copy in sends:
        copy.wait_send()
    when(to, early, "wait_send", range(4))
    when(to, late, "wait_send", range(4))


def per_device(shots, counts, fwd_prev, fwd_cur, adj_late, adj_now, courant, wavelet, boxes, sources, slab_top):
    nz, ny, nx = courant.shape
    f32 = jnp.float32
    smem = pl.BlockSpec(memory_space=pltpu.SMEM)
    hbm = pl.BlockSpec(memory_space=pltpu.HBM)
    out = pl.pallas_call(
        functools.partial(kernel, shots, counts),
        out_shape=jax.ShapeDtypeStruct((nz // 2, nx // 2, ny // 2), f32),
        in_specs=[smem] * 4 + [hbm] * 5,
        out_specs=pl.BlockSpec(memory_space=pltpu.VMEM),
        scratch_shapes=[
            pltpu.VMEM((2, nz, ny + 2 * PAD, nx), f32),
            pltpu.VMEM((2, nz, ny + 2 * PAD, nx), f32),
            pltpu.VMEM((2, nz, ny, nx), f32),
            pltpu.VMEM((nz, ny, nx), f32),
            pltpu.VMEM((nz // 2, ny, nx), f32),
            pltpu.VMEM((2, 2, ny // 4, nx), f32),
            pltpu.VMEM((2, 2, ny // 4, nx), f32),
            pltpu.VMEM((ny // 2, nx), f32),
            pltpu.VMEM((ny // 2, nx), f32),
            pltpu.VMEM((3 * nx, nx), jnp.bfloat16),
            pltpu.VMEM((3 * nx, nx), jnp.bfloat16),
            pltpu.VMEM((nx, ny // 2), f32),
            pltpu.VMEM((max(shots - 1, 1), nx, ny // 2), f32),
            pltpu.SemaphoreType.DMA((5,)),
            pltpu.SemaphoreType.DMA((2, 4)),
            pltpu.SemaphoreType.DMA((2, 4)),
            pltpu.SemaphoreType.DMA((max(shots - 1, 1),)),
            pltpu.SemaphoreType.DMA((max(shots - 1, 1),)),
        ],
        compiler_params=pltpu.CompilerParams(
            collective_id=0, has_side_effects=True, vmem_limit_bytes=54912 * 1024
        ),
    )(wavelet, boxes, sources, slab_top, fwd_prev, fwd_cur, adj_late, adj_now, courant)
    return jnp.swapaxes(out, 1, 2)


def solution(mesh):
    shots = mesh.shape["shot"]
    counts = (mesh.shape["gy"], mesh.shape["gx"])
    return jax.shard_map(
        functools.partial(per_device, shots, counts),
        mesh=mesh,
        in_specs=(
            P("shot", None, "gy", "gx"),
            P("shot", None, "gy", "gx"),
            P("shot", None, "gy", "gx"),
            P("shot", None, "gy", "gx"),
            P(None, "gy", "gx"),
            P("shot", None),
            P("shot", None),
            P("shot", None),
            P(),
        ),
        out_specs=P(None, "gy", "gx"),
        check_vma=False,
    )
```

```python
import functools

import jax
import jax.numpy as jnp
from jax import lax
from jax.experimental import pallas as pl
from jax.experimental.pallas import tpu as pltpu
from jax.sharding import PartitionSpec as P

COEFFS = (-205.0 / 72.0, 8.0 / 5.0, -1.0 / 5.0, 8.0 / 315.0, -1.0 / 560.0)
MESH = pl.DeviceIdType.MESH
PAD = 8
LANES = 128
ROWS = 16


def kernel(
    shots, counts, wave_ref, box_ref, src_ref, top_ref, f0_hbm, f1_hbm, a3_hbm, a2_hbm, c_hbm, out_ref,
    now, mid, old, speed, image, strips_out, strips_in, own, fix, ring, band, coarse, arrived,
    load_sem, send_sem, recv_sem, shot_send, shot_recv,
):
    county, countx = counts
    nz, ny = speed.shape[0], speed.shape[1]
    half, quarter = ny // 2, ny // 4
    planes = [(f, z) for f in range(2) for z in range(nz)]
    gy, gx, shot = lax.axis_index("gy"), lax.axis_index("gx"), lax.axis_index("shot")
    has_up, has_down = gy > 0, gy < county - 1
    has_left, has_right = gx > 0, gx < countx - 1

    loads = [
        pltpu.make_async_copy(f1_hbm.at[0], now.at[0, :, pl.ds(PAD, ny), :], load_sem.at[0]),
        pltpu.make_async_copy(a2_hbm.at[0], now.at[1, :, pl.ds(PAD, ny), :], load_sem.at[1]),
        pltpu.make_async_copy(c_hbm, speed, load_sem.at[2]),
        pltpu.make_async_copy(f0_hbm.at[0], old.at[0], load_sem.at[3]),
        pltpu.make_async_copy(a3_hbm.at[0], old.at[1], load_sem.at[4]),
    ]
    for load in loads:
        load.start()

    barrier = pltpu.get_barrier_semaphore()
    sides = [
        (has_up, {"gy": gy - 1}),
        (has_down, {"gy": gy + 1}),
        (has_left, {"gx": gx - 1}),
        (has_right, {"gx": gx + 1}),
    ]
    for there, device in sides:
        @pl.when(there)
        def _(device=device):
            pl.semaphore_signal(barrier, inc=1, device_id=device, device_id_type=MESH)
    for step in range(1, shots):
        pl.semaphore_signal(
            barrier, inc=1, device_id={"shot": lax.rem(shot + step, shots)}, device_id_type=MESH
        )
    expected = shots - 1
    for there, _ in sides:
        expected = expected + there.astype(jnp.int32)

    nothing = jnp.zeros((2, nz, PAD, LANES), jnp.float32)
    for there, start in ((has_up, 0), (has_down, PAD + ny)):
        @pl.when(jnp.logical_not(there))
        def _(start=start):
            now[:, :, pl.ds(start, PAD), :] = nothing
            mid[:, :, pl.ds(start, PAD), :] = nothing
    for there, side in ((has_left, 0), (has_right, 1)):
        @pl.when(jnp.logical_not(there))
        def _(side=side):
            strips_in[:, side] = jnp.zeros((2, quarter, LANES), jnp.float32)

    lane = lax.broadcasted_iota(jnp.int32, (8, LANES), 1)
    group = lane // 8
    low = lax.rem(lane, 8) < 4
    edge = (lane < 4) | (lane >= LANES - 4)

    ri = lax.broadcasted_iota(jnp.int32, (LANES, LANES), 0)
    ci = lax.broadcasted_iota(jnp.int32, (LANES, LANES), 1)
    apart = jnp.abs(ri - ci)
    around = jnp.minimum(apart, LANES - apart)
    crossing = (ri // 8 == ci // 8) & ((lax.rem(ri, 8) < 4) != (lax.rem(ci, 8) < 4))
    weights = jnp.zeros((LANES, LANES), jnp.float32)
    crossed = weights
    for k in range(1, 5):
        weights = jnp.where(around == k, COEFFS[k], weights)
        crossed = jnp.where(crossing & (apart == k), COEFFS[k], crossed)
    for ref, whole in ((ring, weights), (band, crossed)):
        high = whole.astype(jnp.bfloat16)
        ref[0:LANES] = high
        ref[LANES : 2 * LANES] = high
        ref[2 * LANES : 3 * LANES] = (whole - high.astype(jnp.float32)).astype(jnp.bfloat16)

    def times(x, ref):
        high = x.astype(jnp.bfloat16)
        rest = (x - high.astype(jnp.float32)).astype(jnp.bfloat16)
        return jnp.dot(
            jnp.concatenate([high, rest, high], 1), ref[...], preferred_element_type=jnp.float32
        )

    def stencil(cells, at):
        centre = [cells[f, z, pl.ds(at + PAD, ROWS), :] for f, z in planes]
        along_x = times(jnp.concatenate(centre, 0), ring)
        result = []
        for p, (f, z) in enumerate(planes):
            total = along_x[p * ROWS : (p + 1) * ROWS] + (3.0 * COEFFS[0]) * centre[p]
            for k in range(1, 5):
                s = cells[f, z, pl.ds(at + (PAD + k), ROWS), :]
                s = s + cells[f, z, pl.ds(at + (PAD - k), ROWS), :]
                if z + k < nz:
                    s = s + centre[p + k]
                if z - k >= 0:
                    s = s + centre[p - k]
                total = total + COEFFS[k] * s
            result.append(total)
        return centre, result

    y0, y1, x0, x1 = box_ref[0, 0], box_ref[0, 1], box_ref[0, 2], box_ref[0, 3]
    sz, sy, sx = src_ref[0, 0], src_ref[0, 1], src_ref[0, 2]

    def place(at, rows):
        cell_y = gy * ny + at + lax.broadcasted_iota(jnp.int32, (rows, LANES), 0)
        cell_x = gx * LANES + lax.broadcasted_iota(jnp.int32, (rows, LANES), 1)
        inside = (cell_x >= x0) & (cell_x < x1) & (cell_y >= y0) & (cell_y < y1)
        return inside, (cell_x == sx) & (cell_y == sy)

    def amplitude(step, z):
        return jnp.where(sz == z, wave_ref[0, step], 0.0)

    def first_step(i, carry):
        at = pl.multiple_of(i * ROWS, ROWS)
        here = pl.ds(at, ROWS)
        inside, source = place(at, ROWS)
        centre, lap = stencil(now, at)
        for p, (f, z) in enumerate(planes):
            new = 2.0 * centre[p] - old[f, z, here, :] + speed[z, here, :] * lap[p]
            if f == 0:
                new = new + jnp.where(source, amplitude(0, z), 0.0)
            mid[f, z, pl.ds(at + PAD, ROWS), :] = jnp.where(inside, new, 0.0)
        return carry

    def second_step(i, carry):
        at = pl.multiple_of(i * ROWS, ROWS)
        here, padded = pl.ds(at, ROWS), pl.ds(at + PAD, ROWS)
        inside, source = place(at, ROWS)
        centre, lap = stencil(mid, at)
        total = None
        for z in range(nz):
            c = speed[z, here, :]
            f0, f1, a2 = old[0, z, here, :], now[0, z, padded, :], now[1, z, padded, :]
            f2, a1 = centre[z], centre[nz + z]
            f3 = 2.0 * f2 - f1 + c * lap[z] + jnp.where(source, amplitude(1, z), 0.0)
            f3 = jnp.where(inside, f3, 0.0)
            a0 = jnp.where(inside, 2.0 * a1 - a2 + c * lap[nz + z], 0.0)
            part = a0 * (f2 - 2.0 * f1 + f0) + a1 * (f3 - 2.0 * f2 + f1)
            total = part if z % 2 == 0 else total + part
            if z % 2 == 1:
                image[z // 2, here, :] = total
        return carry

    def spot(i, part, q):
        return pl.multiple_of(i * 8, 8) + (q * half + part * quarter)

    def packing(phase, value):
        def pack(i, carry):
            both = []
            for part in range(2):
                packed = jnp.zeros((8, LANES), jnp.float32)
                for q in range(2):
                    for p, cells in enumerate(value(i, part, q)):
                        base = q * 64 + p * 8
                        moved = pltpu.roll(cells, (base + 4) % LANES, 1)
                        packed = jnp.where(group == base // 8, moved, packed)
                own[pl.ds(pl.multiple_of(i * 8, 8) + part * quarter, 8), :] = packed
                both.append(packed)
            rows = pl.ds(pl.multiple_of(i * 8, 8), 8)
            strips_out[phase, 0, rows, :] = jnp.where(low, both[0], pltpu.roll(both[1], 4, 1))
            strips_out[phase, 1, rows, :] = jnp.where(
                low, pltpu.roll(both[0], LANES - 4, 1), both[1]
            )
            return carry

        lax.fori_loop(0, quarter // 8, pack, 0, unroll=2)

    def plain(i, part, q):
        return [now[f, z, pl.ds(spot(i, part, q) + PAD, 8), :] for f, z in planes]

    def fixes(i, part, q):
        packed = fix[pl.ds(pl.multiple_of(i * 8, 8) + part * quarter, 8), :]
        at = spot(i, part, q)
        inside, _ = place(at, 8)
        result = []
        for p, (f, z) in enumerate(planes):
            moved = pltpu.roll(packed, (124 - q * 64 - p * 8) % LANES, 1)
            result.append(jnp.where(inside & edge, speed[z, pl.ds(at, 8), :] * moved, 0.0))
        return result

    def fixed_middle(i, part, q):
        padded = pl.ds(spot(i, part, q) + PAD, 8)
        result = []
        for (f, z), lack in zip(planes, fixes(i, part, q)):
            value = mid[f, z, padded, :] + lack
            mid[f, z, padded, :] = value
            result.append(value)
        return result

    def fix_image(i, carry):
        for part in range(2):
            for q in range(2):
                at = spot(i, part, q)
                here, padded = pl.ds(at, 8), pl.ds(at + PAD, 8)
                lack = fixes(i, part, q)
                for z in range(0, nz, 2):
                    total = image[z // 2, here, :]
                    for d in (z, z + 1):
                        bent = mid[0, d, padded, :] - 2.0 * now[0, d, padded, :] + old[0, d, here, :]
                        total = total + lack[nz + d] * bent + mid[1, d, padded, :] * lack[d]
                    image[z // 2, here, :] = total
        return carry

    to = (has_down, has_up, has_right, has_left)
    came = (has_up, has_down, has_left, has_right)

    def exchange(cells, phase):
        def remote(index, src, dst, device):
            return pltpu.make_async_remote_copy(
                src_ref=src, dst_ref=dst,
                send_sem=send_sem.at[phase, index], recv_sem=recv_sem.at[phase, index],
                device_id=device, device_id_type=MESH,
            )

        first, last = pl.ds(PAD, PAD), pl.ds(ny, PAD)
        above, below = pl.ds(0, PAD), pl.ds(PAD + ny, PAD)
        return [
            remote(0, cells.at[:, :, last, :], cells.at[:, :, above, :], {"gy": gy + 1}),
            remote(1, cells.at[:, :, first, :], cells.at[:, :, below, :], {"gy": gy - 1}),
            remote(2, strips_out.at[phase, 0], strips_in.at[phase, 0], {"gx": gx + 1}),
            remote(3, strips_out.at[phase, 1], strips_in.at[phase, 1], {"gx": gx - 1}),
        ]

    def when(conditions, copies, action, which):
        for i in which:
            @pl.when(conditions[i])
            def _(i=i):
                getattr(copies[i], action)()

    def merge(phase):
        left, right = strips_in[phase, 0], strips_in[phase, 1]
        few = lax.rem(lax.broadcasted_iota(jnp.int32, (quarter, LANES), 1), 8) < 4
        both = jnp.concatenate(
            [
                jnp.where(few, left, pltpu.roll(right, 4, 1)),
                jnp.where(few, pltpu.roll(left, LANES - 4, 1), right),
            ],
            0,
        )
        fix[...] = times(both - own[...], band)

    chunks = ny // ROWS
    border = chunks - 1
    loads[0].wait()
    loads[1].wait()
    pl.semaphore_wait(barrier, expected)
    early = exchange(now, 0)
    when(to, early, "start", (0, 1))
    packing(0, plain)
    when(to, early, "start", (2, 3))
    for load in loads[2:]:
        load.wait()
    lax.fori_loop(1, border, first_step, 0)
    when(came, early, "wait_recv", range(4))
    merge(0)
    first_step(0, 0)
    first_step(border, 0)
    packing(1, fixed_middle)

    late = exchange(mid, 1)
    when(to, late, "start", (2, 3, 0, 1))
    lax.fori_loop(1, border, second_step, 0)
    when(came, late, "wait_recv", range(4))
    merge(1)
    second_step(0, 0)
    second_step(border, 0)
    lax.fori_loop(0, quarter // 8, fix_image, 0, unroll=4)

    pair = lax.broadcasted_iota(jnp.int32, (LANES, LANES), 0) // 2
    column = lax.broadcasted_iota(jnp.int32, (LANES, LANES), 1)
    total = None
    for k in range(nz // 2):
        rows = image[k, pl.ds(0, half, stride=2), :] + image[k, pl.ds(1, half, stride=2), :]
        pick = (column == pair + 64 * k).astype(jnp.float32)
        part = lax.dot_general(
            pick, rows, (((0,), (1,)), ((), ())),
            precision=lax.Precision.HIGHEST, preferred_element_type=jnp.float32,
        )
        total = part if total is None else total + part
    coarse[...] = total
    sends = []
    for step in range(1, shots):
        copy = pltpu.make_async_remote_copy(
            src_ref=coarse, dst_ref=arrived.at[step - 1],
            send_sem=shot_send.at[step - 1], recv_sem=shot_recv.at[step - 1],
            device_id={"shot": lax.rem(shot + step, shots)}, device_id_type=MESH,
        )
        copy.start()
        sends.append(copy)
    for step, copy in enumerate(sends):
        copy.wait_recv()
        total = total + arrived[step]
    depth = top_ref[0].astype(jnp.float32)
    for k in range(nz // 2):
        factor = (0.25 + (depth + (2.0 * k + 1.0)) / 128.0) * 0.125
        out_ref[k] = total[64 * k : 64 * k + 64] * factor
    for copy in sends:
        copy.wait_send()
    when(to, early, "wait_send", range(4))
    when(to, late, "wait_send", range(4))


def per_device(shots, counts, fwd_prev, fwd_cur, adj_late, adj_now, courant, wavelet, boxes, sources, slab_top):
    nz, ny, nx = courant.shape
    f32 = jnp.float32
    smem = pl.BlockSpec(memory_space=pltpu.SMEM)
    hbm = pl.BlockSpec(memory_space=pltpu.HBM)
    out = pl.pallas_call(
        functools.partial(kernel, shots, counts),
        out_shape=jax.ShapeDtypeStruct((nz // 2, nx // 2, ny // 2), f32),
        in_specs=[smem] * 4 + [hbm] * 5,
        out_specs=pl.BlockSpec(memory_space=pltpu.VMEM),
        scratch_shapes=[
            pltpu.VMEM((2, nz, ny + 2 * PAD, nx), f32),
            pltpu.VMEM((2, nz, ny + 2 * PAD, nx), f32),
            pltpu.VMEM((2, nz, ny, nx), f32),
            pltpu.VMEM((nz, ny, nx), f32),
            pltpu.VMEM((nz // 2, ny, nx), f32),
            pltpu.VMEM((2, 2, ny // 4, nx), f32),
            pltpu.VMEM((2, 2, ny // 4, nx), f32),
            pltpu.VMEM((ny // 2, nx), f32),
            pltpu.VMEM((ny // 2, nx), f32),
            pltpu.VMEM((3 * nx, nx), jnp.bfloat16),
            pltpu.VMEM((3 * nx, nx), jnp.bfloat16),
            pltpu.VMEM((nx, ny // 2), f32),
            pltpu.VMEM((max(shots - 1, 1), nx, ny // 2), f32),
            pltpu.SemaphoreType.DMA((5,)),
            pltpu.SemaphoreType.DMA((2, 4)),
            pltpu.SemaphoreType.DMA((2, 4)),
            pltpu.SemaphoreType.DMA((max(shots - 1, 1),)),
            pltpu.SemaphoreType.DMA((max(shots - 1, 1),)),
        ],
        compiler_params=pltpu.CompilerParams(
            collective_id=0, has_side_effects=True, vmem_limit_bytes=54912 * 1024
        ),
    )(wavelet, boxes, sources, slab_top, fwd_prev, fwd_cur, adj_late, adj_now, courant)
    return jnp.swapaxes(out, 1, 2)


def solution(mesh):
    shots = mesh.shape["shot"]
    counts = (mesh.shape["gy"], mesh.shape["gx"])
    return jax.shard_map(
        functools.partial(per_device, shots, counts),
        mesh=mesh,
        in_specs=(
            P("shot", None, "gy", "gx"),
            P("shot", None, "gy", "gx"),
            P("shot", None, "gy", "gx"),
            P("shot", None, "gy", "gx"),
            P(None, "gy", "gx"),
            P("shot", None),
            P("shot", None),
            P("shot", None),
            P(),
        ),
        out_specs=P(None, "gy", "gx"),
        check_vma=False,
    )
```

```python
import functools

import jax
import jax.numpy as jnp
from jax import lax
from jax.experimental import pallas as pl
from jax.experimental.pallas import tpu as pltpu
from jax.sharding import PartitionSpec as P

COEFFS = (-205.0 / 72.0, 8.0 / 5.0, -1.0 / 5.0, 8.0 / 315.0, -1.0 / 560.0)
MESH = pl.DeviceIdType.MESH
PAD = 8
LANES = 128
ROWS = 16


def kernel(
    shots, counts, wave_ref, box_ref, src_ref, top_ref, f0_hbm, f1_hbm, a3_hbm, a2_hbm, c_hbm, out_ref,
    now, mid, old, speed, image, strips_out, strips_in, own, fix, ring, band, coarse, arrived,
    load_sem, send_sem, recv_sem, shot_send, shot_recv,
):
    county, countx = counts
    nz, ny = speed.shape[0], speed.shape[1]
    half, quarter = ny // 2, ny // 4
    planes = [(f, z) for f in range(2) for z in range(nz)]
    gy, gx, shot = lax.axis_index("gy"), lax.axis_index("gx"), lax.axis_index("shot")
    has_up, has_down = gy > 0, gy < county - 1
    has_left, has_right = gx > 0, gx < countx - 1

    loads = [
        pltpu.make_async_copy(f1_hbm.at[0], now.at[0, :, pl.ds(PAD, ny), :], load_sem.at[0]),
        pltpu.make_async_copy(a2_hbm.at[0], now.at[1, :, pl.ds(PAD, ny), :], load_sem.at[1]),
        pltpu.make_async_copy(c_hbm, speed, load_sem.at[2]),
        pltpu.make_async_copy(f0_hbm.at[0], old.at[0], load_sem.at[3]),
        pltpu.make_async_copy(a3_hbm.at[0], old.at[1], load_sem.at[4]),
    ]
    for load in loads:
        load.start()

    barrier = pltpu.get_barrier_semaphore()
    sides = [
        (has_up, {"gy": gy - 1}),
        (has_down, {"gy": gy + 1}),
        (has_left, {"gx": gx - 1}),
        (has_right, {"gx": gx + 1}),
    ]
    for there, device in sides:
        @pl.when(there)
        def _(device=device):
            pl.semaphore_signal(barrier, inc=1, device_id=device, device_id_type=MESH)
    for step in range(1, shots):
        pl.semaphore_signal(
            barrier, inc=1, device_id={"shot": lax.rem(shot + step, shots)}, device_id_type=MESH
        )
    expected = shots - 1
    for there, _ in sides:
        expected = expected + there.astype(jnp.int32)

    nothing = jnp.zeros((2, nz, PAD, LANES), jnp.float32)
    for there, start in ((has_up, 0), (has_down, PAD + ny)):
        @pl.when(jnp.logical_not(there))
        def _(start=start):
            now[:, :, pl.ds(start, PAD), :] = nothing
            mid[:, :, pl.ds(start, PAD), :] = nothing
    for there, side in ((has_left, 0), (has_right, 1)):
        @pl.when(jnp.logical_not(there))
        def _(side=side):
            strips_in[:, side] = jnp.zeros((2, quarter, LANES), jnp.float32)

    lane = lax.broadcasted_iota(jnp.int32, (8, LANES), 1)
    group = lane // 8
    low = lax.rem(lane, 8) < 4
    edge = (lane < 4) | (lane >= LANES - 4)

    ri = lax.broadcasted_iota(jnp.int32, (LANES, LANES), 0)
    ci = lax.broadcasted_iota(jnp.int32, (LANES, LANES), 1)
    apart = jnp.abs(ri - ci)
    around = jnp.minimum(apart, LANES - apart)
    crossing = (ri // 8 == ci // 8) & ((lax.rem(ri, 8) < 4) != (lax.rem(ci, 8) < 4))
    weights = jnp.zeros((LANES, LANES), jnp.float32)
    crossed = weights
    for k in range(1, 5):
        weights = jnp.where(around == k, COEFFS[k], weights)
        crossed = jnp.where(crossing & (apart == k), COEFFS[k], crossed)
    for ref, whole in ((ring, weights), (band, crossed)):
        high = whole.astype(jnp.bfloat16)
        ref[0:LANES] = high
        ref[LANES : 2 * LANES] = high
        ref[2 * LANES : 3 * LANES] = (whole - high.astype(jnp.float32)).astype(jnp.bfloat16)

    def times(x, ref):
        high = x.astype(jnp.bfloat16)
        rest = (x - high.astype(jnp.float32)).astype(jnp.bfloat16)
        return jnp.dot(
            jnp.concatenate([high, rest, high], 1), ref[...], preferred_element_type=jnp.float32
        )

    def stencil(cells, at):
        centre = [cells[f, z, pl.ds(at + PAD, ROWS), :] for f, z in planes]
        along_x = times(jnp.concatenate(centre, 0), ring)
        result = []
        for p, (f, z) in enumerate(planes):
            total = along_x[p * ROWS : (p + 1) * ROWS] + (3.0 * COEFFS[0]) * centre[p]
            for k in range(1, 5):
                s = cells[f, z, pl.ds(at + (PAD + k), ROWS), :]
                s = s + cells[f, z, pl.ds(at + (PAD - k), ROWS), :]
                if z + k < nz:
                    s = s + centre[p + k]
                if z - k >= 0:
                    s = s + centre[p - k]
                total = total + COEFFS[k] * s
            result.append(total)
        return centre, result

    y0, y1, x0, x1 = box_ref[0, 0], box_ref[0, 1], box_ref[0, 2], box_ref[0, 3]
    sz, sy, sx = src_ref[0, 0], src_ref[0, 1], src_ref[0, 2]

    def place(at, rows):
        cell_y = gy * ny + at + lax.broadcasted_iota(jnp.int32, (rows, LANES), 0)
        cell_x = gx * LANES + lax.broadcasted_iota(jnp.int32, (rows, LANES), 1)
        inside = (cell_x >= x0) & (cell_x < x1) & (cell_y >= y0) & (cell_y < y1)
        return inside, (cell_x == sx) & (cell_y == sy)

    def amplitude(step, z):
        return jnp.where(sz == z, wave_ref[0, step], 0.0)

    def first_step(i, carry):
        at = pl.multiple_of(i * ROWS, ROWS)
        here = pl.ds(at, ROWS)
        inside, source = place(at, ROWS)
        centre, lap = stencil(now, at)
        for p, (f, z) in enumerate(planes):
            new = 2.0 * centre[p] - old[f, z, here, :] + speed[z, here, :] * lap[p]
            if f == 0:
                new = new + jnp.where(source, amplitude(0, z), 0.0)
            mid[f, z, pl.ds(at + PAD, ROWS), :] = jnp.where(inside, new, 0.0)
        return carry

    def second_step(i, carry):
        at = pl.multiple_of(i * ROWS, ROWS)
        here, padded = pl.ds(at, ROWS), pl.ds(at + PAD, ROWS)
        inside, source = place(at, ROWS)
        centre, lap = stencil(mid, at)
        total = None
        for z in range(nz):
            c = speed[z, here, :]
            f0, f1, a2 = old[0, z, here, :], now[0, z, padded, :], now[1, z, padded, :]
            f2, a1 = centre[z], centre[nz + z]
            f3 = 2.0 * f2 - f1 + c * lap[z] + jnp.where(source, amplitude(1, z), 0.0)
            f3 = jnp.where(inside, f3, 0.0)
            a0 = jnp.where(inside, 2.0 * a1 - a2 + c * lap[nz + z], 0.0)
            part = a0 * (f2 - 2.0 * f1 + f0) + a1 * (f3 - 2.0 * f2 + f1)
            total = part if z % 2 == 0 else total + part
            if z % 2 == 1:
                image[z // 2, here, :] = total
        return carry

    def spot(i, part, q):
        return pl.multiple_of(i * 8, 8) + (q * half + part * quarter)

    def packing(phase, value):
        def pack(i, carry):
            both = []
            for part in range(2):
                packed = jnp.zeros((8, LANES), jnp.float32)
                for q in range(2):
                    for p, cells in enumerate(value(i, part, q)):
                        base = q * 64 + p * 8
                        moved = pltpu.roll(cells, (base + 4) % LANES, 1)
                        packed = jnp.where(group == base // 8, moved, packed)
                own[pl.ds(pl.multiple_of(i * 8, 8) + part * quarter, 8), :] = packed
                both.append(packed)
            rows = pl.ds(pl.multiple_of(i * 8, 8), 8)
            strips_out[phase, 0, rows, :] = jnp.where(low, both[0], pltpu.roll(both[1], 4, 1))
            strips_out[phase, 1, rows, :] = jnp.where(
                low, pltpu.roll(both[0], LANES - 4, 1), both[1]
            )
            return carry

        lax.fori_loop(0, quarter // 8, pack, 0, unroll=2)

    def plain(i, part, q):
        return [now[f, z, pl.ds(spot(i, part, q) + PAD, 8), :] for f, z in planes]

    def fixes(i, part, q):
        packed = fix[pl.ds(pl.multiple_of(i * 8, 8) + part * quarter, 8), :]
        at = spot(i, part, q)
        inside, _ = place(at, 8)
        result = []
        for p, (f, z) in enumerate(planes):
            moved = pltpu.roll(packed, (124 - q * 64 - p * 8) % LANES, 1)
            result.append(jnp.where(inside & edge, speed[z, pl.ds(at, 8), :] * moved, 0.0))
        return result

    def fixed_middle(i, part, q):
        padded = pl.ds(spot(i, part, q) + PAD, 8)
        result = []
        for (f, z), lack in zip(planes, fixes(i, part, q)):
            value = mid[f, z, padded, :] + lack
            mid[f, z, padded, :] = value
            result.append(value)
        return result

    def fix_image(i, carry):
        for part in range(2):
            for q in range(2):
                at = spot(i, part, q)
                here, padded = pl.ds(at, 8), pl.ds(at + PAD, 8)
                lack = fixes(i, part, q)
                for z in range(0, nz, 2):
                    total = image[z // 2, here, :]
                    for d in (z, z + 1):
                        bent = mid[0, d, padded, :] - 2.0 * now[0, d, padded, :] + old[0, d, here, :]
                        total = total + lack[nz + d] * bent + mid[1, d, padded, :] * lack[d]
                    image[z // 2, here, :] = total
        return carry

    to = (has_down, has_up, has_right, has_left)
    came = (has_up, has_down, has_left, has_right)

    def exchange(cells, phase):
        def remote(index, src, dst, device):
            return pltpu.make_async_remote_copy(
                src_ref=src, dst_ref=dst,
                send_sem=send_sem.at[phase, index], recv_sem=recv_sem.at[phase, index],
                device_id=device, device_id_type=MESH,
            )

        first, last = pl.ds(PAD, PAD), pl.ds(ny, PAD)
        above, below = pl.ds(0, PAD), pl.ds(PAD + ny, PAD)
        return [
            remote(0, cells.at[:, :, last, :], cells.at[:, :, above, :], {"gy": gy + 1}),
            remote(1, cells.at[:, :, first, :], cells.at[:, :, below, :], {"gy": gy - 1}),
            remote(2, strips_out.at[phase, 0], strips_in.at[phase, 0], {"gx": gx + 1}),
            remote(3, strips_out.at[phase, 1], strips_in.at[phase, 1], {"gx": gx - 1}),
        ]

    def when(conditions, copies, action, which):
        for i in which:
            @pl.when(conditions[i])
            def _(i=i):
                getattr(copies[i], action)()

    def merge(phase):
        left, right = strips_in[phase, 0], strips_in[phase, 1]
        few = lax.rem(lax.broadcasted_iota(jnp.int32, (quarter, LANES), 1), 8) < 4
        both = jnp.concatenate(
            [
                jnp.where(few, left, pltpu.roll(right, 4, 1)),
                jnp.where(few, pltpu.roll(left, LANES - 4, 1), right),
            ],
            0,
        )
        fix[...] = times(both - own[...], band)

    chunks = ny // ROWS
    border = chunks - 1
    loads[0].wait()
    loads[1].wait()
    pl.semaphore_wait(barrier, expected)
    early = exchange(now, 0)
    when(to, early, "start", (0, 1))
    packing(0, plain)
    when(to, early, "start", (2, 3))
    for load in loads[2:]:
        load.wait()
    lax.fori_loop(1, border, first_step, 0)
    when(came, early, "wait_recv", range(4))
    merge(0)
    first_step(0, 0)
    first_step(border, 0)
    packing(1, fixed_middle)

    late = exchange(mid, 1)
    when(to, late, "start", (2, 3, 0, 1))
    lax.fori_loop(1, border, second_step, 0)
    when(came, late, "wait_recv", range(4))
    merge(1)
    second_step(0, 0)
    second_step(border, 0)
    lax.fori_loop(0, quarter // 8, fix_image, 0, unroll=4)

    pair = lax.broadcasted_iota(jnp.int32, (LANES, LANES), 0) // 2
    column = lax.broadcasted_iota(jnp.int32, (LANES, LANES), 1)
    total = None
    for k in range(nz // 2):
        rows = image[k, pl.ds(0, half, stride=2), :] + image[k, pl.ds(1, half, stride=2), :]
        pick = (column == pair + 64 * k).astype(jnp.bfloat16)
        left, part = rows, None
        for _ in range(3):
            piece = left.astype(jnp.bfloat16)
            left = left - piece.astype(jnp.float32)
            term = lax.dot_general(
                pick, piece, (((0,), (1,)), ((), ())), preferred_element_type=jnp.float32
            )
            part = term if part is None else part + term
        total = part if total is None else total + part
    coarse[...] = total
    sends = []
    for step in range(1, shots):
        copy = pltpu.make_async_remote_copy(
            src_ref=coarse, dst_ref=arrived.at[step - 1],
            send_sem=shot_send.at[step - 1], recv_sem=shot_recv.at[step - 1],
            device_id={"shot": lax.rem(shot + step, shots)}, device_id_type=MESH,
        )
        copy.start()
        sends.append(copy)
    for step, copy in enumerate(sends):
        copy.wait_recv()
        total = total + arrived[step]
    depth = top_ref[0].astype(jnp.float32)
    for k in range(nz // 2):
        factor = (0.25 + (depth + (2.0 * k + 1.0)) / 128.0) * 0.125
        out_ref[k] = total[64 * k : 64 * k + 64] * factor
    for copy in sends:
        copy.wait_send()
    when(to, early, "wait_send", range(4))
    when(to, late, "wait_send", range(4))


def per_device(shots, counts, fwd_prev, fwd_cur, adj_late, adj_now, courant, wavelet, boxes, sources, slab_top):
    nz, ny, nx = courant.shape
    f32 = jnp.float32
    smem = pl.BlockSpec(memory_space=pltpu.SMEM)
    hbm = pl.BlockSpec(memory_space=pltpu.HBM)
    out = pl.pallas_call(
        functools.partial(kernel, shots, counts),
        out_shape=jax.ShapeDtypeStruct((nz // 2, nx // 2, ny // 2), f32),
        in_specs=[smem] * 4 + [hbm] * 5,
        out_specs=pl.BlockSpec(memory_space=pltpu.VMEM),
        scratch_shapes=[
            pltpu.VMEM((2, nz, ny + 2 * PAD, nx), f32),
            pltpu.VMEM((2, nz, ny + 2 * PAD, nx), f32),
            pltpu.VMEM((2, nz, ny, nx), f32),
            pltpu.VMEM((nz, ny, nx), f32),
            pltpu.VMEM((nz // 2, ny, nx), f32),
            pltpu.VMEM((2, 2, ny // 4, nx), f32),
            pltpu.VMEM((2, 2, ny // 4, nx), f32),
            pltpu.VMEM((ny // 2, nx), f32),
            pltpu.VMEM((ny // 2, nx), f32),
            pltpu.VMEM((3 * nx, nx), jnp.bfloat16),
            pltpu.VMEM((3 * nx, nx), jnp.bfloat16),
            pltpu.VMEM((nx, ny // 2), f32),
            pltpu.VMEM((max(shots - 1, 1), nx, ny // 2), f32),
            pltpu.SemaphoreType.DMA((5,)),
            pltpu.SemaphoreType.DMA((2, 4)),
            pltpu.SemaphoreType.DMA((2, 4)),
            pltpu.SemaphoreType.DMA((max(shots - 1, 1),)),
            pltpu.SemaphoreType.DMA((max(shots - 1, 1),)),
        ],
        compiler_params=pltpu.CompilerParams(
            collective_id=0, has_side_effects=True, vmem_limit_bytes=54912 * 1024
        ),
    )(wavelet, boxes, sources, slab_top, fwd_prev, fwd_cur, adj_late, adj_now, courant)
    return jnp.swapaxes(out, 1, 2)


def solution(mesh):
    shots = mesh.shape["shot"]
    counts = (mesh.shape["gy"], mesh.shape["gx"])
    return jax.shard_map(
        functools.partial(per_device, shots, counts),
        mesh=mesh,
        in_specs=(
            P("shot", None, "gy", "gx"),
            P("shot", None, "gy", "gx"),
            P("shot", None, "gy", "gx"),
            P("shot", None, "gy", "gx"),
            P(None, "gy", "gx"),
            P("shot", None),
            P("shot", None),
            P("shot", None),
            P(),
        ),
        out_specs=P(None, "gy", "gx"),
        check_vma=False,
    )
```
